32 devices in a mesh: owner: 4 (over z), tok: 4 (over y, x), rep: 2 (over core).
Axes of the slice: x: 2, y: 2, z: 4, core: 2. Of those that a mesh axis runs over, the one named last changes fastest.
Arguments:
- tokens: bfloat16 [8192, 4096], P(('owner', 'rep'), 'tok'), may hold values from -6 to 6
- frozen_weight: bfloat16 [4096, 4096], P('tok'), may hold values from -0.09375 to 0.09375
- adapter_down: bfloat16 [400, 64, 4096], P('owner', None, 'tok'), may hold values from -0.09375 to 0.09375
- adapter_up: bfloat16 [400, 64, 4096], P('owner', None, 'tok'), may hold values from -0.75 to 0.75
- cotangent: bfloat16 [8192, 4096], P(('owner', 'rep'), 'tok'), may hold values from -6 to 6
- family_ids: int32 [64], replicated, may hold values from 0 to 399, as said below
Outputs:
- projected: bfloat16 [8192, 4096], P(('owner', 'rep'), 'tok')
- grad_input: bfloat16 [8192, 4096], P(('owner', 'rep'), 'tok')
- grad_down: float32 [400, 64, 4096], P('owner', 'rep', 'tok')
- grad_up: float32 [400, 64, 4096], P('owner', 'rep', 'tok')
The draws below stay inside these ranges and needn't reach their ends.
Inputs may be any that keep to these rules, and one draw needn't show every extreme that they name: `family_ids`: block b is held by owner index b // (8 * 2) and rep index (b // 8) % 2. Family f belongs to owner f // 100. Among the 8 blocks of one owner index and one rep index, at most 2 name families of any one owner, and at least one owner has exactly 2 of them.
All inputs are finite; a program needn't handle non-finite values.
Results may differ from the reference program's by a relative error of at most 0.0046.
Values may be sent and summed in bfloat16 or wider, within the bound.
A program may use at most 256 MiB of HBM per device.

```python
import jax
import jax.numpy as jnp
from jax import lax

D = 4096
R = 64
FAM = 400
BLK = 128
CAP = 2
NB = 8
FAM_OWN = 100
TOKENS = 8192
NBLK = 64


def draw_family_ids(key, part):
    group_count = NBLK // NB
    owner_count = FAM // FAM_OWN
    perm_key, first_key, second_key = jax.random.split(key, 3)
    group_keys = jax.random.split(perm_key, group_count)
    owner_perms = jax.vmap(lambda k: jax.random.permutation(k, owner_count))(group_keys)
    pick = jnp.arange(NB, dtype=jnp.int32) // CAP
    owners = jnp.take(owner_perms, pick, axis=1).astype(jnp.int32)
    first = jax.random.randint(first_key, (group_count, NB), 0, FAM_OWN)
    second = jax.random.randint(second_key, (group_count, NB), 0, FAM_OWN)
    local = jnp.minimum(first, second).astype(jnp.int32)
    return (owners * FAM_OWN + local).reshape(-1).astype(jnp.int32)


def levels(own_key, shape, cuts, least, largest):
    level, own = 1.0, jax.random.fold_in(own_key, 6)
    for position, shards_of in cuts:
        draws = jnp.exp(jax.random.uniform(jax.random.fold_in(own, position), (shards_of,), jnp.float32, least / len(cuts), largest / len(cuts)))
        level = level * jnp.repeat(draws, shape[position] // shards_of).reshape([-1 if axis == position else 1 for axis in range(len(shape))])
    return level


def bell_draw(own_key, dims, width, bound, shards=(), kind=jnp.bfloat16):
    loudness = levels(own_key, dims, shards, -0.22, 0.18) if shards else 1.0
    entries = jax.random.normal(own_key, dims, jnp.float32) * width * loudness
    return jnp.minimum(jnp.maximum(entries, -bound), bound).astype(kind)


def setup_inputs(seed: int = 0) -> dict:
    keys = jax.random.split(jax.random.key(seed), 7)
    tokens = bell_draw(keys[0], (TOKENS, D), 1.0, 6.0, ((0, 8), (1, 4)))
    frozen_weight = bell_draw(keys[1], (D, D), D ** -0.5, 0.09375, ((0, 4),))
    adapter_down = bell_draw(keys[2], (FAM, R, D), D ** -0.5, 0.09375, ((0, 4), (2, 4)))
    adapter_up = bell_draw(keys[3], (FAM, R, D), R ** -0.5, 0.75, ((0, 4), (2, 4)))
    cotangent = bell_draw(keys[4], (TOKENS, D), 1.0, 6.0, ((0, 8), (1, 4)))
    family_ids = draw_family_ids(jax.random.fold_in(keys[6], 71), 0)
    return {"tokens": tokens, "frozen_weight": frozen_weight, "adapter_down": adapter_down, "adapter_up": adapter_up, "cotangent": cotangent, "family_ids": family_ids}


adapter_scale = 2.0


def reference(tokens, frozen_weight, adapter_down, adapter_up, cotangent, family_ids):
    block_count = family_ids.shape[0]
    token_blocks = tokens.reshape(block_count, BLK, D).astype(jnp.float32)
    cot_blocks = cotangent.reshape(block_count, BLK, D).astype(jnp.float32)
    down_panels = jnp.take(adapter_down, family_ids, axis=0).astype(jnp.float32)
    up_panels = jnp.take(adapter_up, family_ids, axis=0).astype(jnp.float32)
    low_rank = jnp.einsum("btd,brd->btr", token_blocks, down_panels)
    low_rank = lax.optimization_barrier(low_rank.astype(jnp.bfloat16)).astype(jnp.float32)
    base = jnp.dot(tokens, frozen_weight, preferred_element_type=jnp.float32)
    extra = jnp.einsum("btr,brd->btd", low_rank, up_panels).reshape(-1, D)
    projected = (base + adapter_scale * extra).astype(jnp.bfloat16)
    grad_low = adapter_scale * jnp.einsum("btd,brd->btr", cot_blocks, up_panels)
    grad_low = lax.optimization_barrier(grad_low.astype(jnp.bfloat16)).astype(jnp.float32)
    back = jnp.dot(cotangent, frozen_weight.T, preferred_element_type=jnp.float32)
    back_extra = jnp.einsum("btr,brd->btd", grad_low, down_panels).reshape(-1, D)
    grad_input = (back + back_extra).astype(jnp.bfloat16)
    up_terms = adapter_scale * jnp.einsum("btr,btd->brd", low_rank, cot_blocks)
    down_terms = jnp.einsum("btr,btd->brd", grad_low, token_blocks)
    grad_down = jax.ops.segment_sum(down_terms, family_ids, num_segments=FAM)
    grad_up = jax.ops.segment_sum(up_terms, family_ids, num_segments=FAM)
    return projected, grad_input, grad_down, grad_up
```

```python
import functools

import jax
import jax.numpy as jnp
from jax import lax
from jax.experimental import pallas as pl
from jax.experimental.pallas import tpu as pltpu
from jax.sharding import PartitionSpec as P

BLK = 128
CAP = 2


adapter_scale = 2.0
F32 = jnp.float32
BF16 = jnp.bfloat16


def slot_order(homes):
    count = homes.shape[-1]
    same = homes[..., :, None] == homes[..., None, :]
    iota = jnp.arange(count, dtype=jnp.int32)
    lower = iota[None, :] < iota[:, None]
    return jnp.sum((same & lower).astype(jnp.int32), axis=-1)


def swap(x, axis, size, step):
    return lax.ppermute(x, axis, [(i, i ^ step) for i in range(size)])


def dot_nt(a, b):
    return lax.dot_general(a, b, (((1,), (1,)), ((), ())), preferred_element_type=F32)


def dot_tn(a, b):
    return lax.dot_general(a, b, (((0,), (0,)), ((), ())), preferred_element_type=F32)


def gather_kernel(ids, down_ref, up_ref, out_ref):
    out_ref[0, 0, 0] = down_ref[0]
    out_ref[0, 1, 0] = up_ref[0]


def gather_panels(ids, down, up, n_owner):
    rank, cols = down.shape[1:]
    spec = pl.BlockSpec((1, rank, cols), lambda i, ids: (ids[i], 0, 0))
    return pl.pallas_call(
        gather_kernel,
        grid_spec=pltpu.PrefetchScalarGridSpec(
            num_scalar_prefetch=1,
            grid=(n_owner * CAP,),
            in_specs=[spec, spec],
            out_specs=pl.BlockSpec(
                (1, 2, 1, rank, cols), lambda i, ids: (i // CAP, 0, i % CAP, 0, 0)
            ),
        ),
        out_shape=jax.ShapeDtypeStruct((n_owner, 2, CAP, rank, cols), BF16),
        name="gather_panels",
    )(ids, down, up)


def low_kernel(place, tok_ref, cot_ref, pan_ref, out_ref):
    rank = pan_ref.shape[3]
    out_ref[:, :rank] = dot_nt(tok_ref[...], pan_ref[0, 0, 0])
    out_ref[:, rank:] = adapter_scale * dot_nt(cot_ref[...], pan_ref[0, 1, 0])


def panel_spec(rank, cols):
    return pl.BlockSpec(
        (1, 2, 1, rank, cols), lambda j, place: (place[0, j], 0, place[1, j], 0, 0)
    )


def low_parts(place, tokens, cot, panels):
    rank, cols = panels.shape[3:]
    rows = tokens.shape[0]
    row_spec = pl.BlockSpec((BLK, cols), lambda j, place: (j, 0))
    return pl.pallas_call(
        low_kernel,
        grid_spec=pltpu.PrefetchScalarGridSpec(
            num_scalar_prefetch=1,
            grid=(rows // BLK,),
            in_specs=[row_spec, row_spec, panel_spec(rank, cols)],
            out_specs=pl.BlockSpec((BLK, 2 * rank), lambda j, place: (j, 0)),
        ),
        out_shape=jax.ShapeDtypeStruct((rows, 2 * rank), F32),
        name="low_parts",
    )(place, tokens, cot, panels)


def term_kernel(place, low_ref, tok_ref, cot_ref, out_ref):
    half = out_ref.shape[4]
    n_rep = out_ref.shape[1]
    rank = half * n_rep
    rep = place[2, 0]
    down_terms = dot_tn(low_ref[:, rank:], tok_ref[...])
    up_terms = adapter_scale * dot_tn(low_ref[:, :rank], cot_ref[...])
    for h in range(n_rep):
        where = rep ^ h
        out_ref[0, where, 0, 0] = down_terms[h * half : (h + 1) * half].astype(BF16)
        out_ref[0, where, 0, 1] = up_terms[h * half : (h + 1) * half].astype(BF16)


def grad_terms(place, low, tokens, cot, n_owner, n_rep):
    rows, cols = tokens.shape
    rank = low.shape[1] // 2
    half = rank // n_rep
    row_spec = pl.BlockSpec((BLK, cols), lambda j, place: (j, 0))
    return pl.pallas_call(
        term_kernel,
        grid_spec=pltpu.PrefetchScalarGridSpec(
            num_scalar_prefetch=1,
            grid=(rows // BLK,),
            in_specs=[
                pl.BlockSpec((BLK, 2 * rank), lambda j, place: (j, 0)),
                row_spec,
                row_spec,
            ],
            out_specs=pl.BlockSpec(
                (1, n_rep, 1, 2, half, cols),
                lambda j, place: (place[0, j], 0, place[1, j], 0, 0, 0),
            ),
        ),
        out_shape=jax.ShapeDtypeStruct((n_owner, n_rep, CAP, 2, half, cols), BF16),
        name="grad_terms",
    )(place, low, tokens, cot)


def scatter_kernel(fams, recv_ref, down_ref, up_ref):
    step = down_ref.shape[0]
    base = pl.program_id(0) * step
    down_ref[...] = jnp.zeros_like(down_ref)
    up_ref[...] = jnp.zeros_like(up_ref)
    for s in range(recv_ref.shape[0]):
        spot = fams[s] - base

        @pl.when((spot >= 0) & (spot < step))
        def _():
            down_ref[spot] += recv_ref[s, 0].astype(F32)
            up_ref[spot] += recv_ref[s, 1].astype(F32)


def scatter_families(fams, recv, fam_own):
    half, cols = recv.shape[2:]
    step = next(s for s in (10, 5, 4, 2, 1) if fam_own % s == 0)
    out_spec = pl.BlockSpec((step, half, cols), lambda i, fams: (i, 0, 0))
    shape = jax.ShapeDtypeStruct((fam_own, half, cols), F32)
    return pl.pallas_call(
        scatter_kernel,
        grid_spec=pltpu.PrefetchScalarGridSpec(
            num_scalar_prefetch=1,
            grid=(fam_own // step,),
            in_specs=[pl.BlockSpec(recv.shape, lambda i, fams: (0, 0, 0, 0))],
            out_specs=[out_spec, out_spec],
        ),
        out_shape=[shape, shape],
        name="scatter_families",
    )(fams, recv)


def finish_kernel(kind, count, place, low_ref, pan_ref, own_ref, *refs):
    recvs, out_ref = refs[:count], refs[count]
    rank = pan_ref.shape[3]
    if kind == 1:
        total = adapter_scale * jnp.dot(
            low_ref[:, :rank], pan_ref[0, 1, 0], preferred_element_type=F32
        )
    else:
        total = jnp.dot(low_ref[:, rank:], pan_ref[0, 0, 0], preferred_element_type=F32)
    total += own_ref[...]
    for r in recvs:
        total += r[...].astype(F32)
    out_ref[...] = total.astype(BF16)


def finish(kind, place, low, panels, own, recvs):
    rank, cols = panels.shape[3:]
    rows = own.shape[0]
    row_spec = pl.BlockSpec((BLK, cols), lambda j, place: (j, 0))
    return pl.pallas_call(
        functools.partial(finish_kernel, kind, len(recvs)),
        grid_spec=pltpu.PrefetchScalarGridSpec(
            num_scalar_prefetch=1,
            grid=(rows // BLK,),
            in_specs=[
                pl.BlockSpec((BLK, 2 * rank), lambda j, place: (j, 0)),
                panel_spec(rank, cols),
                row_spec,
            ]
            + [row_spec] * len(recvs),
            out_specs=row_spec,
        ),
        out_shape=jax.ShapeDtypeStruct((rows, cols), BF16),
        name=("finish_back", "finish_out")[kind],
    )(place, low, panels, own, *recvs)


def tables(family_ids, owner, rep, n_owner, n_rep, fam_own):
    fam = family_ids.reshape(n_owner, n_rep, -1)
    homes = fam // fam_own
    slots = slot_order(homes)
    cap_iota = jnp.arange(CAP, dtype=jnp.int32)
    hit = (homes == owner)[..., None] & (slots[..., None] == cap_iota)
    local = fam - owner * fam_own
    sent = jnp.sum(jnp.where(hit, local[..., None] + 1, 0), axis=2) - 1
    o_iota = jnp.arange(n_owner, dtype=jnp.int32)
    r_iota = jnp.arange(n_rep, dtype=jnp.int32)
    o_sel = (o_iota[:, None] ^ owner) == o_iota[None, :]
    r_sel = (r_iota[:, None] ^ rep) == r_iota[None, :]
    pick = o_sel[:, None, :, None] & r_sel[None, :, None, :]
    rel = jnp.sum(jnp.where(pick[..., None], sent[None, None], 0), axis=(2, 3))
    mine = (o_iota == owner)[:, None, None] & (r_iota == rep)[None, :, None]
    my_home = jnp.sum(jnp.where(mine, homes, 0), axis=(0, 1))
    my_slot = jnp.sum(jnp.where(mine, slots, 0), axis=(0, 1))
    place = jnp.stack([my_home ^ owner, my_slot, jnp.full_like(my_slot, rep)])
    return rel.astype(jnp.int32), place.astype(jnp.int32)


def shards(tokens, frozen_weight, adapter_down, adapter_up, cotangent, family_ids):
    n_owner, n_tok, n_rep = (lax.axis_size(a) for a in ("owner", "tok", "rep"))
    owner, tok, rep = (lax.axis_index(a) for a in ("owner", "tok", "rep"))
    rows, cols = tokens.shape
    fam_own = adapter_down.shape[0]
    inner = 1 << ((n_tok.bit_length() - 1) // 2)
    outer = n_tok // inner
    b = tok % inner

    rel, place = tables(family_ids, owner, rep, n_owner, n_rep, fam_own)

    send = gather_panels(
        jnp.maximum(rel[:, 0], 0).reshape(-1), adapter_down, adapter_up, n_owner
    )
    panels = jnp.stack(
        [send[0]] + [swap(send[s], "owner", n_owner, s) for s in range(1, n_owner)]
    )

    quarter = cols // (2 * n_rep)
    parity = owner % 2
    row_at = (rep * 2 + parity) * quarter
    cot_rel = [cotangent] + [
        swap(cotangent, "tok", n_tok, ar * inner) for ar in range(1, outer)
    ]
    weight_rel = []
    first = []
    for br in range(inner):
        col_at = [(((tok // inner) ^ ar) * inner + (b ^ br)) * cols for ar in range(outer)]
        if br == 0:
            weight_rel.append(
                [lax.dynamic_slice(frozen_weight, (0, at), (cols, cols)) for at in col_at]
            )
            continue
        piece = jnp.concatenate(
            [lax.dynamic_slice(frozen_weight, (row_at, at), (quarter, cols)) for at in col_at]
        )
        first.append(swap(piece, "tok", n_tok, br))
    if first:
        tokens_after, first = lax.optimization_barrier((tokens, first))
    tok_rel = [tokens] + [swap(tokens_after, "tok", n_tok, br) for br in range(1, inner)]
    for piece in first:
        other = swap(piece, "owner", n_owner, 1)
        lo = jnp.where(parity == 0, piece, other)
        hi = jnp.where(parity == 0, other, piece)
        mine = jnp.stack([lo, hi])
        theirs = swap(mine, "rep", n_rep, 1)
        both = [jnp.where(rep == r, mine, theirs) for r in range(n_rep)]
        weight_rel.append(
            [
                jnp.concatenate(
                    [
                        both[r][e, ar * quarter : (ar + 1) * quarter]
                        for r in range(n_rep)
                        for e in range(2)
                    ]
                )
                for ar in range(outer)
            ]
        )

    part = low_parts(place, tokens, cotangent, panels)
    piece_rows = rows // n_tok

    def rows_of(x, t):
        return lax.dynamic_slice_in_dim(x, t * piece_rows, piece_rows, 0)

    total = rows_of(part, tok)
    for s in range(1, n_tok):
        total = total + swap(rows_of(part, tok ^ s), "tok", n_tok, s)
    total = total.astype(BF16)
    low = jnp.zeros((rows, part.shape[1]), BF16)
    for s in range(n_tok):
        got = swap(total, "tok", n_tok, s) if s else total
        low = lax.dynamic_update_slice_in_dim(low, got, (tok ^ s) * piece_rows, 0)

    terms = grad_terms(place, low, tokens, cotangent, n_owner, n_rep)
    recv = []
    for s in range(n_owner):
        for rs in range(n_rep):
            term = terms[s, rs]
            if s or rs:
                term = lax.ppermute(
                    term,
                    ("owner", "rep"),
                    [
                        (o * n_rep + r, (o ^ s) * n_rep + (r ^ rs))
                        for o in range(n_owner)
                        for r in range(n_rep)
                    ],
                )
            recv.append(term)
    recv = jnp.concatenate(recv)
    grad_down, grad_up = scatter_families(rel.reshape(-1), recv, fam_own)

    def back_of(br):
        acc = None
        for ar in range(outer):
            d = dot_nt(cot_rel[ar], weight_rel[br][ar])
            acc = d if acc is None else acc + d
        return acc

    back_recv = [swap(back_of(br).astype(BF16), "tok", n_tok, br) for br in range(1, inner)]

    def base_of(ar):
        acc = None
        for br in range(inner):
            d = jnp.dot(tok_rel[br], weight_rel[br][ar], preferred_element_type=F32)
            acc = d if acc is None else acc + d
        return acc

    base_recv = [
        swap(base_of(ar).astype(BF16), "tok", n_tok, ar * inner) for ar in range(1, outer)
    ]
    grad_input = finish(0, place, low, panels, back_of(0), back_recv)
    projected = finish(1, place, low, panels, base_of(0), base_recv)
    return (projected, grad_input, grad_down, grad_up)


def solution(mesh):
    in_specs = (
        P(("owner", "rep"), "tok"),
        P("tok", None),
        P("owner", None, "tok"),
        P("owner", None, "tok"),
        P(("owner", "rep"), "tok"),
        P(),
    )
    out_specs = (
        P(("owner", "rep"), "tok"),
        P(("owner", "rep"), "tok"),
        P("owner", "rep", "tok"),
        P("owner", "rep", "tok"),
    )
    return jax.shard_map(shards, mesh=mesh, in_specs=in_specs, out_specs=out_specs, check_vma=False)
```

```python
import functools

import jax
import jax.numpy as jnp
from jax import lax
from jax.experimental import pallas as pl
from jax.experimental.pallas import tpu as pltpu
from jax.sharding import PartitionSpec as P


BLK = 128
CAP = 2


adapter_scale = 2.0
F32 = jnp.float32
BF16 = jnp.bfloat16


def slot_order(homes):
    count = homes.shape[-1]
    same = homes[..., :, None] == homes[..., None, :]
    iota = jnp.arange(count, dtype=jnp.int32)
    lower = iota[None, :] < iota[:, None]
    return jnp.sum((same & lower).astype(jnp.int32), axis=-1)


def swap(x, axis, size, step):
    return lax.ppermute(x, axis, [(i, i ^ step) for i in range(size)])


def dot_nt(a, b):
    return lax.dot_general(a, b, (((1,), (1,)), ((), ())), preferred_element_type=F32)


def dot_tn(a, b):
    return lax.dot_general(a, b, (((0,), (0,)), ((), ())), preferred_element_type=F32)


def gather_kernel(ids, table_ref, out_ref):
    out_ref[...] = table_ref[...]


def gather_panels(ids, table, n_owner):
    rank, cols = table.shape[1:]
    spec = pl.BlockSpec((1, rank, cols), lambda i, ids: (ids[i], 0, 0))
    out = pl.pallas_call(
        gather_kernel,
        grid_spec=pltpu.PrefetchScalarGridSpec(
            num_scalar_prefetch=1,
            grid=(n_owner * CAP,),
            in_specs=[spec],
            out_specs=pl.BlockSpec((1, rank, cols), lambda i, ids: (i, 0, 0)),
        ),
        out_shape=jax.ShapeDtypeStruct((n_owner * CAP, rank, cols), BF16),
    )(ids, table)
    return out.reshape(n_owner, CAP, rank, cols)


def panel_spec(rank, cols, step=1, at=0):
    return pl.BlockSpec(
        (1, 1, rank, cols),
        lambda j, place: (place[0, j * step + at], place[1, j * step + at], 0, 0),
    )


def low_kernel(scale, place, x_ref, pan_ref, out_ref):
    out_ref[...] = scale * dot_nt(x_ref[...], pan_ref[0, 0])


def low_parts(scale, place, x, panels):
    rank, cols = panels.shape[2:]
    rows = x.shape[0]
    return pl.pallas_call(
        functools.partial(low_kernel, scale),
        grid_spec=pltpu.PrefetchScalarGridSpec(
            num_scalar_prefetch=1,
            grid=(rows // BLK,),
            in_specs=[
                pl.BlockSpec((BLK, cols), lambda j, place: (j, 0)),
                panel_spec(rank, cols),
            ],
            out_specs=pl.BlockSpec((BLK, rank), lambda j, place: (j, 0)),
        ),
        out_shape=jax.ShapeDtypeStruct((rows, rank), F32),
    )(place, x, panels)


def term_kernel(scale, place, low_ref, x_ref, out_ref):
    n_rep, _, half = out_ref.shape[1:4]
    rep = place[2, 0]
    terms = (scale * dot_tn(low_ref[...], x_ref[...])).astype(BF16)
    for h in range(n_rep):
        out_ref[0, rep ^ h, 0] = terms[h * half : (h + 1) * half]


def grad_terms(scale, place, low, x, n_owner, n_rep):
    rows, cols = x.shape
    rank = low.shape[1]
    half = rank // n_rep
    return pl.pallas_call(
        functools.partial(term_kernel, scale),
        grid_spec=pltpu.PrefetchScalarGridSpec(
            num_scalar_prefetch=1,
            grid=(rows // BLK,),
            in_specs=[
                pl.BlockSpec((BLK, rank), lambda j, place: (j, 0)),
                pl.BlockSpec((BLK, cols), lambda j, place: (j, 0)),
            ],
            out_specs=pl.BlockSpec(
                (1, n_rep, 1, half, cols),
                lambda j, place: (place[0, j], 0, place[1, j], 0, 0),
            ),
        ),
        out_shape=jax.ShapeDtypeStruct((n_owner, n_rep, CAP, half, cols), BF16),
    )(place, low, x)


def scatter_kernel(fams, *refs):
    out_ref = refs[-1]
    step = out_ref.shape[0]
    base = pl.program_id(0) * step
    out_ref[...] = jnp.zeros_like(out_ref)
    for k, recv_ref in enumerate(refs[:-1]):
        for c in range(CAP):
            spot = fams[k * CAP + c] - base

            @pl.when((spot >= 0) & (spot < step))
            def _(recv_ref=recv_ref, c=c, spot=spot):
                out_ref[spot] += recv_ref[c].astype(F32)


def scatter_families(fams, recvs, fam_own):
    half, cols = recvs[0].shape[1:]
    step = next(s for s in (20, 10, 5, 4, 2, 1) if fam_own % s == 0)
    return pl.pallas_call(
        scatter_kernel,
        grid_spec=pltpu.PrefetchScalarGridSpec(
            num_scalar_prefetch=1,
            grid=(fam_own // step,),
            in_specs=[pl.BlockSpec(recvs[0].shape, lambda i, fams: (0, 0, 0))] * len(recvs),
            out_specs=pl.BlockSpec((step, half, cols), lambda i, fams: (i, 0, 0)),
        ),
        out_shape=jax.ShapeDtypeStruct((fam_own, half, cols), F32),
    )(fams, *recvs)


def own_kernel(dot, scale, group, count, place, low_ref, *refs):
    pans, xs, ws = refs[:group], refs[group : group + count], refs[group + count : -1]
    out_ref = refs[-1]
    total = dot(xs[0][...], ws[0][...])
    for x, w in zip(xs[1:], ws[1:]):
        total += dot(x[...], w[...])
    for g in range(group):
        at = slice(g * BLK, (g + 1) * BLK)
        extra = jnp.dot(low_ref[at], pans[g][0, 0], preferred_element_type=F32)
        out_ref[at] = total[at] + scale * extra


def own_sums(dot, scale, place, low, panels, xs, ws):
    rank, cols = panels.shape[2:]
    rows = xs[0].shape[0]
    group = 2 if rows % (2 * BLK) == 0 else 1
    height = group * BLK
    row_spec = pl.BlockSpec((height, cols), lambda j, place: (j, 0))
    return pl.pallas_call(
        functools.partial(own_kernel, dot, scale, group, len(xs)),
        grid_spec=pltpu.PrefetchScalarGridSpec(
            num_scalar_prefetch=1,
            grid=(rows // height,),
            in_specs=[pl.BlockSpec((height, rank), lambda j, place: (j, 0))]
            + [panel_spec(rank, cols, group, g) for g in range(group)]
            + [row_spec] * len(xs)
            + [pl.BlockSpec(ws[0].shape, lambda j, place: (0, 0))] * len(ws),
            out_specs=row_spec,
        ),
        out_shape=jax.ShapeDtypeStruct((rows, cols), F32),
    )(place, low, *[panels] * group, *xs, *ws)


def dot_nn(a, b):
    return jnp.dot(a, b, preferred_element_type=F32)


def tables(family_ids, owner, rep, n_owner, n_rep, fam_own):
    fam = family_ids.reshape(n_owner, n_rep, -1)
    homes = fam // fam_own
    slots = slot_order(homes)
    cap_iota = jnp.arange(CAP, dtype=jnp.int32)
    hit = (homes == owner)[..., None] & (slots[..., None] == cap_iota)
    local = fam - owner * fam_own
    sent = jnp.sum(jnp.where(hit, local[..., None] + 1, 0), axis=2) - 1
    o_iota = jnp.arange(n_owner, dtype=jnp.int32)
    r_iota = jnp.arange(n_rep, dtype=jnp.int32)
    o_sel = (o_iota[:, None] ^ owner) == o_iota[None, :]
    r_sel = (r_iota[:, None] ^ rep) == r_iota[None, :]
    pick = o_sel[:, None, :, None] & r_sel[None, :, None, :]
    rel = jnp.sum(jnp.where(pick[..., None], sent[None, None], 0), axis=(2, 3))
    mine = (o_iota == owner)[:, None, None] & (r_iota == rep)[None, :, None]
    my_home = jnp.sum(jnp.where(mine, homes, 0), axis=(0, 1))
    my_slot = jnp.sum(jnp.where(mine, slots, 0), axis=(0, 1))
    place = jnp.stack([my_home ^ owner, my_slot, jnp.full_like(my_slot, rep)])
    return rel.astype(jnp.int32), place.astype(jnp.int32)


def shards(tokens, frozen_weight, adapter_down, adapter_up, cotangent, family_ids):
    n_owner, n_tok, n_rep = (lax.axis_size(a) for a in ("owner", "tok", "rep"))
    owner, tok, rep = (lax.axis_index(a) for a in ("owner", "tok", "rep"))
    rows, cols = tokens.shape
    fam_own = adapter_down.shape[0]
    inner = 1 << ((n_tok.bit_length() - 1) // 2)
    outer = n_tok // inner
    b = tok % inner

    cot_rel = [cotangent] + [
        swap(cotangent, "tok", n_tok, ar * inner) for ar in range(1, outer)
    ]

    quarter = cols // (2 * n_rep)
    parity = owner % 2
    row_at = (rep * 2 + parity) * quarter
    weight_rel = []
    first = []
    for br in range(inner):
        col_at = [(((tok // inner) ^ ar) * inner + (b ^ br)) * cols for ar in range(outer)]
        if br == 0:
            weight_rel.append(
                [lax.dynamic_slice(frozen_weight, (0, at), (cols, cols)) for at in col_at]
            )
            continue
        piece = jnp.concatenate(
            [lax.dynamic_slice(frozen_weight, (row_at, at), (quarter, cols)) for at in col_at]
        )
        first.append(swap(piece, "tok", n_tok, br))

    rel, place = tables(family_ids, owner, rep, n_owner, n_rep, fam_own)
    ids = jnp.maximum(rel[:, 0], 0).reshape(-1)

    def fetch(send):
        return [send[0]] + [
            swap(send[s], "owner", n_owner, s) for s in range(1, n_owner)
        ]

    send_down = gather_panels(ids, adapter_down, n_owner)
    send_up = gather_panels(ids, adapter_up, n_owner)
    got_down = fetch(send_down)
    got_down, send_up = lax.optimization_barrier((got_down, send_up))
    got_up = fetch(send_up)
    down_panels = jnp.stack(got_down)
    up_panels = jnp.stack(got_up)

    tokens_after = tokens
    if first:
        tokens_after, first = lax.optimization_barrier((tokens, first))
    tok_rel = [tokens] + [
        swap(tokens_after, "tok", n_tok, br) for br in range(1, inner)
    ]
    for piece in first:
        other = swap(piece, "owner", n_owner, 1)
        lo = jnp.where(parity == 0, piece, other)
        hi = jnp.where(parity == 0, other, piece)
        mine = jnp.stack([lo, hi])
        theirs = swap(mine, "rep", n_rep, 1)
        both = [jnp.where(rep == r, mine, theirs) for r in range(n_rep)]
        weight_rel.append(
            [
                jnp.concatenate(
                    [
                        both[r][e, ar * quarter : (ar + 1) * quarter]
                        for r in range(n_rep)
                        for e in range(2)
                    ]
                )
                for ar in range(outer)
            ]
        )

    piece_rows = rows // n_tok

    def rows_of(x, t):
        return lax.dynamic_slice_in_dim(x, t * piece_rows, piece_rows, 0)

    def sum_tok(part):
        total = rows_of(part, tok)
        for s in range(1, n_tok):
            total = total + swap(rows_of(part, tok ^ s), "tok", n_tok, s)
        total = total.astype(BF16)
        low = jnp.zeros(part.shape, BF16)
        for s in range(n_tok):
            got = swap(total, "tok", n_tok, s) if s else total
            low = lax.dynamic_update_slice_in_dim(low, got, (tok ^ s) * piece_rows, 0)
        return low

    def to_owners(terms):
        recvs = []
        for s in range(n_owner):
            for rs in range(n_rep):
                term = terms[s, rs]
                if s or rs:
                    pairs = [
                        (o * n_rep + r, (o ^ s) * n_rep + (r ^ rs))
                        for o in range(n_owner)
                        for r in range(n_rep)
                    ]
                    term = lax.ppermute(term, ("owner", "rep"), pairs)
                recvs.append(term)
        return recvs

    fams = rel.reshape(-1)
    low = sum_tok(low_parts(1.0, place, tokens, down_panels))
    up_terms = grad_terms(adapter_scale, place, low, cotangent, n_owner, n_rep)
    up_recv = to_owners(up_terms)
    grad_low = sum_tok(low_parts(adapter_scale, place, cotangent, up_panels))
    down_terms = grad_terms(1.0, place, grad_low, tokens, n_owner, n_rep)
    down_recv = to_owners(down_terms)

    def partial(dot, xs, ws):
        acc = None
        for x, w in zip(xs, ws):
            d = dot(x, w)
            acc = d if acc is None else acc + d
        return acc.astype(BF16)

    back_recv = [
        swap(partial(dot_nt, cot_rel, weight_rel[br]), "tok", n_tok, br)
        for br in range(1, inner)
    ]
    base_recv = [
        swap(
            partial(dot_nn, tok_rel, [w[ar] for w in weight_rel]),
            "tok", n_tok, ar * inner,
        )
        for ar in range(1, outer)
    ]
    back = own_sums(dot_nt, 1.0, place, grad_low, down_panels, cot_rel, weight_rel[0])
    base = own_sums(
        dot_nn, adapter_scale, place, low, up_panels, tok_rel,
        [w[0] for w in weight_rel],
    )
    grad_up = scatter_families(fams, up_recv, fam_own)
    grad_down = scatter_families(fams, down_recv, fam_own)

    def finish(own, recvs):
        for r in recvs:
            own = own + r.astype(F32)
        return own.astype(BF16)

    return (finish(base, base_recv), finish(back, back_recv), grad_down, grad_up)


def solution(mesh):
    in_specs = (
        P(("owner", "rep"), "tok"),
        P("tok", None),
        P("owner", None, "tok"),
        P("owner", None, "tok"),
        P(("owner", "rep"), "tok"),
        P(),
    )
    out_specs = (
        P(("owner", "rep"), "tok"),
        P(("owner", "rep"), "tok"),
        P("owner", "rep", "tok"),
        P("owner", "rep", "tok"),
    )

    return jax.shard_map(
        shards, mesh=mesh, in_specs=in_specs, out_specs=out_specs, check_vma=False
    )
```

```python
import functools

import jax
import jax.numpy as jnp
from jax import lax
from jax.experimental import pallas as pl
from jax.experimental.pallas import tpu as pltpu
from jax.sharding import PartitionSpec as P


BLK = 128
CAP = 2


adapter_scale = 2.0
F32 = jnp.float32
BF16 = jnp.bfloat16


def slot_order(homes):
    count = homes.shape[-1]
    same = homes[..., :, None] == homes[..., None, :]
    iota = jnp.arange(count, dtype=jnp.int32)
    lower = iota[None, :] < iota[:, None]
    return jnp.sum((same & lower).astype(jnp.int32), axis=-1)


def swap(x, axis, size, step):
    return lax.ppermute(x, axis, [(i, i ^ step) for i in range(size)])


def dot_nt(a, b):
    return lax.dot_general(a, b, (((1,), (1,)), ((), ())), preferred_element_type=F32)


def dot_tn(a, b):
    return lax.dot_general(a, b, (((0,), (0,)), ((), ())), preferred_element_type=F32)


def gather_kernel(count, ids, *refs):
    for k in range(count):
        refs[count][k] = refs[k][0]


def gather_panels(ids, table, n_owner):
    rank, cols = table.shape[1:]
    count = n_owner * CAP
    specs = [
        pl.BlockSpec((1, rank, cols), lambda i, ids, k=k: (ids[k], 0, 0)) for k in range(count)
    ]
    out = pl.pallas_call(
        functools.partial(gather_kernel, count),
        grid_spec=pltpu.PrefetchScalarGridSpec(
            num_scalar_prefetch=1,
            grid=(1,),
            in_specs=specs,
            out_specs=pl.BlockSpec((count, rank, cols), lambda i, ids: (0, 0, 0)),
        ),
        out_shape=jax.ShapeDtypeStruct((count, rank, cols), BF16),
    )(ids, *[table] * count)
    return out.reshape(n_owner, CAP, rank, cols)


def panel_spec(rank, cols, step=1, at=0):
    return pl.BlockSpec(
        (1, 1, rank, cols),
        lambda j, place: (place[0, j * step + at], place[1, j * step + at], 0, 0),
    )


def whole_spec(shape):
    return pl.BlockSpec(shape, lambda i, place: (0,) * len(shape))


def low_kernel(scale, place, x_ref, pan_ref, out_ref):
    for j in range(x_ref.shape[0] // BLK):
        at = slice(j * BLK, (j + 1) * BLK)
        panel = pan_ref[place[0, j], place[1, j]]
        out_ref[at] = scale * dot_nt(x_ref[at], panel)


def low_parts(scale, place, x, panels):
    out_shape = (x.shape[0], panels.shape[2])
    return pl.pallas_call(
        functools.partial(low_kernel, scale),
        grid_spec=pltpu.PrefetchScalarGridSpec(
            num_scalar_prefetch=1,
            grid=(1,),
            in_specs=[whole_spec(x.shape), whole_spec(panels.shape)],
            out_specs=whole_spec(out_shape),
        ),
        out_shape=jax.ShapeDtypeStruct(out_shape, F32),
    )(place, x, panels)


def term_kernel(scale, place, low_ref, x_ref, out_ref):
    n_rep, _, half = out_ref.shape[1:4]
    rep = place[2, 0]
    for j in range(x_ref.shape[0] // BLK):
        at = slice(j * BLK, (j + 1) * BLK)
        terms = (scale * dot_tn(low_ref[at], x_ref[at])).astype(BF16)
        for h in range(n_rep):
            out_ref[place[0, j], rep ^ h, place[1, j]] = terms[h * half : (h + 1) * half]


def grad_terms(scale, place, low, x, n_owner, n_rep):
    cols = x.shape[1]
    half = low.shape[1] // n_rep
    out_shape = (n_owner, n_rep, CAP, half, cols)
    return pl.pallas_call(
        functools.partial(term_kernel, scale),
        grid_spec=pltpu.PrefetchScalarGridSpec(
            num_scalar_prefetch=1,
            grid=(1,),
            in_specs=[whole_spec(low.shape), whole_spec(x.shape)],
            out_specs=whole_spec(out_shape),
        ),
        out_shape=jax.ShapeDtypeStruct(out_shape, BF16),
    )(place, low, x)


def scatter_kernel(fams, *refs):
    out_ref = refs[-1]
    step = out_ref.shape[0]
    base = pl.program_id(0) * step
    out_ref[...] = jnp.zeros_like(out_ref)
    for k, recv_ref in enumerate(refs[:-1]):
        for c in range(CAP):
            spot = fams[k * CAP + c] - base

            @pl.when((spot >= 0) & (spot < step))
            def _(recv_ref=recv_ref, c=c, spot=spot):
                out_ref[spot] += recv_ref[c].astype(F32)


def scatter_families(fams, recvs, fam_own):
    half, cols = recvs[0].shape[1:]
    step = next(s for s in (20, 10, 5, 4, 2, 1) if fam_own % s == 0)
    return pl.pallas_call(
        scatter_kernel,
        grid_spec=pltpu.PrefetchScalarGridSpec(
            num_scalar_prefetch=1,
            grid=(fam_own // step,),
            in_specs=[pl.BlockSpec(recvs[0].shape, lambda i, fams: (0, 0, 0))] * len(recvs),
            out_specs=pl.BlockSpec((step, half, cols), lambda i, fams: (i, 0, 0)),
        ),
        out_shape=jax.ShapeDtypeStruct((fam_own, half, cols), F32),
    )(fams, *recvs)


def own_kernel(dot, scale, group, count, place, low_ref, *refs):
    pans, xs, ws = refs[:group], refs[group : group + count], refs[group + count : -1]
    out_ref = refs[-1]
    total = dot(xs[0][...], ws[0][...])
    for x, w in zip(xs[1:], ws[1:]):
        total += dot(x[...], w[...])
    for g in range(group):
        at = slice(g * BLK, (g + 1) * BLK)
        extra = jnp.dot(low_ref[at], pans[g][0, 0], preferred_element_type=F32)
        out_ref[at] = total[at] + scale * extra


def own_sums(dot, scale, place, low, panels, xs, ws):
    rank, cols = panels.shape[2:]
    rows = xs[0].shape[0]
    group = 2 if rows % (2 * BLK) == 0 else 1
    height = group * BLK
    row_spec = pl.BlockSpec((height, cols), lambda j, place: (j, 0))
    return pl.pallas_call(
        functools.partial(own_kernel, dot, scale, group, len(xs)),
        grid_spec=pltpu.PrefetchScalarGridSpec(
            num_scalar_prefetch=1,
            grid=(rows // height,),
            in_specs=[pl.BlockSpec((height, rank), lambda j, place: (j, 0))]
            + [panel_spec(rank, cols, group, g) for g in range(group)]
            + [row_spec] * len(xs)
            + [pl.BlockSpec(ws[0].shape, lambda j, place: (0, 0))] * len(ws),
            out_specs=row_spec,
        ),
        out_shape=jax.ShapeDtypeStruct((rows, cols), F32),
    )(place, low, *[panels] * group, *xs, *ws)


def dot_nn(a, b):
    return jnp.dot(a, b, preferred_element_type=F32)


def tables(family_ids, owner, rep, n_owner, n_rep, fam_own):
    fam = family_ids.reshape(n_owner, n_rep, -1)
    homes = fam // fam_own
    slots = slot_order(homes)
    cap_iota = jnp.arange(CAP, dtype=jnp.int32)
    hit = (homes == owner)[..., None] & (slots[..., None] == cap_iota)
    local = fam - owner * fam_own
    sent = jnp.sum(jnp.where(hit, local[..., None] + 1, 0), axis=2) - 1
    o_iota = jnp.arange(n_owner, dtype=jnp.int32)
    r_iota = jnp.arange(n_rep, dtype=jnp.int32)
    o_sel = (o_iota[:, None] ^ owner) == o_iota[None, :]
    r_sel = (r_iota[:, None] ^ rep) == r_iota[None, :]
    pick = o_sel[:, None, :, None] & r_sel[None, :, None, :]
    rel = jnp.sum(jnp.where(pick[..., None], sent[None, None], 0), axis=(2, 3))
    mine = (o_iota == owner)[:, None, None] & (r_iota == rep)[None, :, None]
    my_home = jnp.sum(jnp.where(mine, homes, 0), axis=(0, 1))
    my_slot = jnp.sum(jnp.where(mine, slots, 0), axis=(0, 1))
    place = jnp.stack([my_home ^ owner, my_slot, jnp.full_like(my_slot, rep)])
    return rel.astype(jnp.int32), place.astype(jnp.int32)


def shards(tokens, frozen_weight, adapter_down, adapter_up, cotangent, family_ids):
    n_owner, n_tok, n_rep = (lax.axis_size(a) for a in ("owner", "tok", "rep"))
    owner, tok, rep = (lax.axis_index(a) for a in ("owner", "tok", "rep"))
    rows, cols = tokens.shape
    fam_own = adapter_down.shape[0]
    inner = 1 << ((n_tok.bit_length() - 1) // 2)
    outer = n_tok // inner
    b = tok % inner

    cot_rel = [cotangent] + [swap(cotangent, "tok", n_tok, ar * inner) for ar in range(1, outer)]

    quarter = cols // (2 * n_rep)
    parity = owner % 2
    row_at = (rep * 2 + parity) * quarter
    weight_rel = []
    first = []
    for br in range(inner):
        col_at = [(((tok // inner) ^ ar) * inner + (b ^ br)) * cols for ar in range(outer)]
        if br == 0:
            weight_rel.append(
                [lax.dynamic_slice(frozen_weight, (0, at), (cols, cols)) for at in col_at]
            )
            continue
        piece = jnp.concatenate(
            [lax.dynamic_slice(frozen_weight, (row_at, at), (quarter, cols)) for at in col_at]
        )
        first.append(swap(piece, "tok", n_tok, br))

    rel, place = tables(family_ids, owner, rep, n_owner, n_rep, fam_own)
    ids = jnp.maximum(rel[:, 0], 0).reshape(-1)

    def fetch(send):
        return [send[0]] + [swap(send[s], "owner", n_owner, s) for s in range(1, n_owner)]

    send_down = gather_panels(ids, adapter_down, n_owner)
    send_up = gather_panels(ids, adapter_up, n_owner)
    got_down = fetch(send_down)
    got_down, send_up = lax.optimization_barrier((got_down, send_up))
    got_up = fetch(send_up)
    down_panels = jnp.stack(got_down)
    up_panels = jnp.stack(got_up)

    tokens_after = tokens
    if first:
        tokens_after, first = lax.optimization_barrier((tokens, first))
    tok_rel = [tokens] + [swap(tokens_after, "tok", n_tok, br) for br in range(1, inner)]
    for piece in first:
        other = swap(piece, "owner", n_owner, 1)
        lo = jnp.where(parity == 0, piece, other)
        hi = jnp.where(parity == 0, other, piece)
        mine = jnp.stack([lo, hi])
        theirs = swap(mine, "rep", n_rep, 1)
        both = [jnp.where(rep == r, mine, theirs) for r in range(n_rep)]
        weight_rel.append(
            [
                jnp.concatenate(
                    [
                        both[r][e, ar * quarter : (ar + 1) * quarter]
                        for r in range(n_rep)
                        for e in range(2)
                    ]
                )
                for ar in range(outer)
            ]
        )

    piece_rows = rows // n_tok

    def rows_of(x, t):
        return lax.dynamic_slice_in_dim(x, t * piece_rows, piece_rows, 0)

    def sum_tok(part):
        total = rows_of(part, tok)
        for s in range(1, n_tok):
            total = total + swap(rows_of(part, tok ^ s), "tok", n_tok, s)
        total = total.astype(BF16)
        low = jnp.zeros(part.shape, BF16)
        for s in range(n_tok):
            got = swap(total, "tok", n_tok, s) if s else total
            low = lax.dynamic_update_slice_in_dim(low, got, (tok ^ s) * piece_rows, 0)
        return low

    def to_owners(terms):
        recvs = []
        for s in range(n_owner):
            for rs in range(n_rep):
                term = terms[s, rs]
                if s or rs:
                    pairs = [
                        (o * n_rep + r, (o ^ s) * n_rep + (r ^ rs))
                        for o in range(n_owner)
                        for r in range(n_rep)
                    ]
                    term = lax.ppermute(term, ("owner", "rep"), pairs)
                recvs.append(term)
        return recvs

    fams = rel.reshape(-1)
    low = sum_tok(low_parts(1.0, place, tokens, down_panels))
    up_terms = grad_terms(adapter_scale, place, low, cotangent, n_owner, n_rep)
    up_recv = to_owners(up_terms)
    grad_low = sum_tok(low_parts(adapter_scale, place, cotangent, up_panels))
    down_terms = grad_terms(1.0, place, grad_low, tokens, n_owner, n_rep)
    down_recv = to_owners(down_terms)

    def partial(dot, xs, ws):
        acc = None
        for x, w in zip(xs, ws):
            d = dot(x, w)
            acc = d if acc is None else acc + d
        return acc.astype(BF16)

    back_recv = [
        swap(partial(dot_nt, cot_rel, weight_rel[br]), "tok", n_tok, br)
        for br in range(1, inner)
    ]
    base_recv = [
        swap(
            partial(dot_nn, tok_rel, [w[ar] for w in weight_rel]),
            "tok", n_tok, ar * inner,
        )
        for ar in range(1, outer)
    ]
    back = own_sums(dot_nt, 1.0, place, grad_low, down_panels, cot_rel, weight_rel[0])
    base = own_sums(
        dot_nn, adapter_scale, place, low, up_panels, tok_rel,
        [w[0] for w in weight_rel],
    )
    grad_up = scatter_families(fams, up_recv, fam_own)
    grad_down = scatter_families(fams, down_recv, fam_own)

    def finish(own, recvs):
        for r in recvs:
            own = own + r.astype(F32)
        return own.astype(BF16)

    return (finish(base, base_recv), finish(back, back_recv), grad_down, grad_up)


def solution(mesh):
    in_specs = (
        P(("owner", "rep"), "tok"),
        P("tok", None),
        P("owner", None, "tok"),
        P("owner", None, "tok"),
        P(("owner", "rep"), "tok"),
        P(),
    )
    out_specs = (
        P(("owner", "rep"), "tok"),
        P(("owner", "rep"), "tok"),
        P("owner", "rep", "tok"),
        P("owner", "rep", "tok"),
    )

    return jax.shard_map(shards, mesh=mesh, in_specs=in_specs, out_specs=out_specs, check_vma=False)
```
